256 devices in a mesh: row: 16 (over y, z_lo, core), col: 16 (over x, z_hi).
Axes of the slice: x: 4, y: 4, z: 8 (z_hi: 4, z_lo: 2; z = z_hi * 2 + z_lo), core: 2. Of those that a mesh axis runs over, the one named last changes fastest.
Arguments:
- features: bfloat16 [16, 4096, 128], P('col', 'row'), may hold values from -6 to 6
- block_values: bfloat16 [16, 16, 320, 128, 128], P('row', 'col'), may hold values from -0.078125 to 0.078125
- block_row: int32 [16, 16, 320], P('row', 'col'), may hold values from 0 to 31
- block_col: int32 [16, 16, 320], P('row', 'col'), may hold values from 0 to 31
- block_occupancy: int32 [16, 16], P('row', 'col'), may hold values from 40 to 320, as said below
- weight: bfloat16 [128, 128], replicated, may hold values from -0.5 to 0.5
- cotangent: bfloat16 [16, 4096, 128], P('row', 'col'), may hold values from -6 to 6
Outputs:
- out_features: bfloat16 [16, 4096, 128], P('row', 'col')
- weight_grad: float32 [128, 128], replicated
- feature_grad: bfloat16 [16, 4096, 128], P('col', 'row')
The draws below stay inside these ranges and needn't reach their ends.
Inputs may be any that keep to these rules, and one draw needn't show every extreme that they name: `block_occupancy`: live slots of one tile name distinct blocks; some tile has all 320 slots live in every draw.
All inputs are finite; a program needn't handle non-finite values.
Results may differ from the reference program's by a relative error of at most 0.005.
Values may be sent and summed in bfloat16 or wider, within the bound.
A program may use at most 192 MiB of HBM per device.

```python
import math
import jax
import jax.numpy as jnp
from jax import lax

F = 128
BLK = 128
NODES = 65536
ROWBLK = 4096
COLBLK = 4096
BROWS = 32
BCOLS = 32
NB = 320
N_ROW = 16
N_COL = 16


def tile_pattern(key):
    tile_count = N_ROW * N_COL
    slot_total = BROWS * BCOLS
    lowest = max(1, NB // 8)
    middle = max(lowest, NB // 2)
    base_key, heavy_key, pick_key, perm_key, top_key = jax.random.split(jax.random.fold_in(key, 7), 5)
    base_counts = jax.random.randint(base_key, (tile_count,), lowest, middle + 1)
    heavy_counts = jax.random.randint(heavy_key, (tile_count,), middle, NB + 1)
    heavy_pick = jax.random.randint(pick_key, (tile_count,), 0, 16) == 0
    counts = jnp.where(heavy_pick, heavy_counts, base_counts)
    top_tile = jax.random.randint(top_key, (), 0, tile_count)
    counts = jnp.where(jnp.arange(tile_count) == top_tile, NB, counts)
    tile_keys = jax.random.split(perm_key, tile_count)
    chosen = jax.vmap(lambda one_key: jax.random.permutation(one_key, slot_total)[:NB])(tile_keys)
    owned_rows_lookup = (chosen // BCOLS).astype(jnp.int32).reshape(N_ROW, N_COL, NB)
    cols_of = (chosen % BCOLS).astype(jnp.int32).reshape(N_ROW, N_COL, NB)
    return (counts.astype(jnp.int32).reshape(N_ROW, N_COL), owned_rows_lookup, cols_of)


def draw_block_occupancy(key, part):
    return tile_pattern(key)[0]


def draw_block_row(key, part):
    return tile_pattern(key)[1]


def draw_block_col(key, part):
    return tile_pattern(key)[2]


def shard_levels(rng, dims, pieces, low, high):
    factor_of = 1.0
    for dim, shards_of in pieces:
        draws = jax.random.uniform(jax.random.fold_in(jax.random.fold_in(rng, 6), dim), (shards_of,), jnp.float32, low / len(pieces), high / len(pieces))
        factor_of = factor_of * jnp.repeat(jnp.exp(draws), dims[dim] // shards_of).reshape((-1,) + (1,) * (len(dims) - 1 - dim))
    return factor_of


def normal_values(key, dims, deviation, limit, cuts=(), kind=jnp.bfloat16):
    drawn = jax.random.normal(key, dims, jnp.float32) * deviation
    if len(cuts) > 0:
        drawn = shard_levels(key, dims, cuts, -0.22, 0.18) * drawn
    return jnp.clip(drawn, min=-limit, max=limit).astype(kind)


def setup_inputs(seed: int = 0) -> dict:
    key_list = jax.random.split(jax.random.key(seed), 8)
    return {
        "features": normal_values(key_list[0], (N_COL, COLBLK, F), 1.0, 6.0, ((0, 16), (1, 16))),
        "block_values": normal_values(key_list[1], (N_ROW, N_COL, NB, BLK, BLK), (max(BLK, BLK * NB * N_COL // (3 * BROWS))) ** -0.5, 0.078125, ((0, 16), (1, 16))),
        "block_row": draw_block_row(jax.random.fold_in(key_list[7], 71), 0),
        "block_col": draw_block_col(jax.random.fold_in(key_list[7], 71), 0),
        "block_occupancy": draw_block_occupancy(jax.random.fold_in(key_list[7], 71), 0),
        "weight": normal_values(key_list[5], (F, F), F ** -0.5, 0.5),
        "cotangent": normal_values(key_list[6], (N_ROW, ROWBLK, F), 1.0, 6.0, ((0, 16), (1, 16))),
    }


def reference(features, block_values, block_row, block_col, block_occupancy, weight, cotangent):
    tile_count = N_ROW * N_COL
    tile_entries = block_values.reshape(tile_count, NB, BLK, BLK)
    tile_rows = block_row.reshape(tile_count, NB)
    tile_cols = block_col.reshape(tile_count, NB)
    tile_live = block_occupancy.reshape(tile_count)
    slot_index = jnp.arange(NB, dtype=jnp.int32)
    row_range = jnp.arange(BROWS, dtype=jnp.int32)
    col_range = jnp.arange(BCOLS, dtype=jnp.int32)
    tile_ids = jnp.arange(tile_count, dtype=jnp.int32)

    def forward(totals, tile_item):
        tile_id, values, owned_rows_lookup, cols_of, live_count = tile_item
        row_tile = tile_id // N_COL
        col_tile = tile_id % N_COL
        column_rows = lax.dynamic_index_in_dim(features, col_tile, 0, keepdims=False)
        picked = column_rows.reshape(BCOLS, BLK, F)[cols_of].astype(jnp.float32)
        tile_multiplied = jnp.einsum('sab,sbf->saf', values.astype(jnp.float32), picked, precision=lax.Precision.HIGHEST)
        live_mask = (slot_index < live_count).astype(jnp.float32)
        select_rows = (owned_rows_lookup[:, None] == row_range[None, :]).astype(jnp.float32) * live_mask[:, None]
        partial_output = jnp.einsum('sr,saf->raf', select_rows, tile_multiplied, precision=lax.Precision.HIGHEST)
        return (totals.at[row_tile].add(partial_output.reshape(ROWBLK, F)), None)
    agg_sum = lax.scan(forward, jnp.zeros((N_ROW, ROWBLK, F), jnp.float32), (tile_ids, tile_entries, tile_rows, tile_cols, tile_live))[0]
    neighbor_total = agg_sum.astype(jnp.bfloat16).reshape(NODES, F)
    out_features = jnp.dot(neighbor_total, weight, preferred_element_type=jnp.float32).astype(jnp.bfloat16)
    cot_flat = cotangent.reshape(NODES, F)
    weight_grad = jnp.dot(neighbor_total.T, cot_flat, preferred_element_type=jnp.float32) * (1.0 / math.sqrt(NODES))
    grad_agg = jnp.dot(cot_flat, weight.T, preferred_element_type=jnp.float32).astype(jnp.bfloat16)
    grad_tiles = grad_agg.reshape(N_ROW, BROWS, BLK, F)

    def backward(totals, tile_item):
        tile_id, values, owned_rows_lookup, cols_of, live_count = tile_item
        row_tile = tile_id // N_COL
        col_tile = tile_id % N_COL
        grad_rows = lax.dynamic_index_in_dim(grad_tiles, row_tile, 0, keepdims=False)
        picked = grad_rows[owned_rows_lookup].astype(jnp.float32)
        tile_multiplied = jnp.einsum('sab,saf->sbf', values.astype(jnp.float32), picked, precision=lax.Precision.HIGHEST)
        live_mask = (slot_index < live_count).astype(jnp.float32)
        gather_columns = (cols_of[:, None] == col_range[None, :]).astype(jnp.float32) * live_mask[:, None]
        partial_output = jnp.einsum('wx,wyn->xyn', gather_columns, tile_multiplied, precision=lax.Precision.HIGHEST)
        return (totals.at[col_tile].add(partial_output.reshape(COLBLK, F)), None)
    grad_sum = lax.scan(backward, jnp.zeros((N_COL, COLBLK, F), jnp.float32), (tile_ids, tile_entries, tile_rows, tile_cols, tile_live))[0]
    feature_grad = grad_sum.astype(jnp.bfloat16)
    return (out_features.reshape(N_ROW, ROWBLK, F), weight_grad, feature_grad)
```

```python
import functools
import math

import jax
import jax.numpy as jnp
from jax import lax
from jax.experimental import pallas as pl
from jax.experimental.pallas import tpu as pltpu
from jax.sharding import PartitionSpec as P

MESH = pl.DeviceIdType.MESH
F32 = jnp.float32
BF16 = jnp.bfloat16
VM = pl.BlockSpec(memory_space=pltpu.VMEM)
UNROLL = 8


def place():
    r, c = lax.axis_index("row"), lax.axis_index("col")
    return r // 4, (r // 2) % 2, r % 2, c // 4, c % 4


def device(where, dy=0, dl=0, dc=0, dx=0, dz=0):
    y, l, k, x, z = where
    row = ((y + dy + 4) % 4) * 4 + ((l + dl) % 2) * 2 + (k + dc) % 2
    col = ((x + dx + 4) % 4) * 4 + (z + dz + 4) % 4
    return (row, col)


def meet(peers):
    barrier = pltpu.get_barrier_semaphore()
    for peer in peers:
        pl.semaphore_signal(barrier, inc=1, device_id=peer, device_id_type=MESH)
    pl.semaphore_wait(barrier, len(peers))


class Mail:
    def __init__(self, send_sems, recv_sems):
        self.send_sems, self.recv_sems = send_sems, recv_sems
        self.copies, self.waiting = {}, {}

    def send(self, key, src, dst, peer):
        i = len(self.copies)
        copy = pltpu.make_async_remote_copy(
            src_ref=src,
            dst_ref=dst,
            send_sem=self.send_sems.at[i],
            recv_sem=self.recv_sems.at[i],
            device_id=peer,
            device_id_type=MESH,
        )
        copy.start()
        self.copies[key] = copy
        self.waiting[key] = copy

    def take(self, *keys):
        for key in keys:
            if key in self.waiting:
                self.waiting.pop(key).wait_recv()

    def finish(self):
        self.take(*list(self.waiting))
        for copy in self.copies.values():
            copy.wait_send()


GATHER_COPIES = 6 + 24 + 1 + 12 + 8


def gather_kernel(f_ref, c_ref, fall, call, send_sems, recv_sems):
    where = place()
    y, l, k, x, z = where
    dev = functools.partial(device, where)
    xp, xm, zp, zm = dev(dx=1), dev(dx=-1), dev(dz=1), dev(dz=-1)
    yp, ym, lo, other = dev(dy=1), dev(dy=-1), dev(dl=1), dev(dc=1)
    meet([xp, xm, zp, zm, yp, ym, lo, other])
    mail = Mail(send_sems, recv_sems)

    def cat(dx, dz, h):
        return call.at[(((x + dx + 4) % 4) * 4 + (z + dz + 4) % 4) * 2 + h]

    def fat(dy, dl, h):
        return fall.at[(((y + dy + 4) % 4) * 4 + ((l + dl) % 2) * 2 + k) * 2 + h]

    def fboth(dy, dl):
        return fall.at[pl.ds((((y + dy + 4) % 4) * 4 + ((l + dl) % 2) * 2 + k) * 2, 2)]

    def xsend(d, h, p):
        src = c_ref.at[h] if d == 0 else cat(0, d, h)
        mail.send(("x", d, h, p), src, cat(0, d, h), xp if p > 0 else xm)

    def zsend(h, p):
        mail.send(("z", h, p), c_ref.at[h], cat(0, 0, h), zp if p > 0 else zm)

    def ysend(e, h, p):
        src = f_ref.at[h] if e == 0 else fat(0, e, h)
        mail.send(("y", e, h, p), src, fat(0, e, h), yp if p > 0 else ym)

    def xrelay(d):
        mail.take(("x", d, 0, 1))
        mail.send(("xr", d, 1), cat(-1, d, 0), cat(-1, d, 0), xp)
        mail.take(("x", d, 1, -1))
        mail.send(("xr", d, -1), cat(1, d, 1), cat(1, d, 1), xm)

    def yrelay(e):
        mail.take(("y", e, 0, 1))
        mail.send(("yr", e, 1), fat(-1, e, 0), fat(-1, e, 0), yp)
        mail.take(("y", e, 1, -1))
        mail.send(("yr", e, -1), fat(1, e, 1), fat(1, e, 1), ym)

    def share(dy, dl):
        src = f_ref if (dy, dl) == (0, 0) else fboth(dy, dl)
        mail.send(("k", dy, dl), src, fboth(dy, dl), other)

    for h, p in ((0, 1), (1, -1), (1, 1), (0, -1)):
        zsend(h, p)
        xsend(0, h, p)
        if (h, p) == (0, 1):
            mail.send(("l",), f_ref, fboth(0, 0), lo)
        ysend(0, h, p)
    share(0, 0)
    call[pl.ds(((x * 4) + z) * 2, 2)] = c_ref[...]
    fall[pl.ds((y * 4 + l * 2 + k) * 2, 2)] = f_ref[...]

    xrelay(0)
    yrelay(0)
    mail.take(("l",))
    for h, p in ((0, 1), (1, -1), (1, 1), (0, -1)):
        ysend(1, h, p)
    mail.take(("z", 0, 1))
    mail.send(("zr", 1), cat(0, -1, 0), cat(0, -1, 0), zp)
    xsend(-1, 0, 1)
    xsend(-1, 0, -1)
    mail.take(("z", 1, -1))
    mail.send(("zr", -1), cat(0, 1, 1), cat(0, 1, 1), zm)
    xsend(1, 1, 1)
    xsend(1, 1, -1)
    mail.take(("z", 1, 1))
    xsend(-1, 1, 1)
    xsend(-1, 1, -1)
    mail.take(("z", 0, -1))
    xsend(1, 0, 1)
    xsend(1, 0, -1)
    share(0, 1)
    mail.take(("y", 0, 1, 1))
    share(-1, 0)
    mail.take(("y", 0, 0, -1))
    share(1, 0)
    yrelay(1)
    xrelay(-1)
    mail.take(("zr", 1))
    xsend(2, 0, 1)
    xsend(2, 0, -1)
    mail.take(("zr", -1))
    xsend(2, 1, 1)
    xsend(2, 1, -1)
    xrelay(1)
    mail.take(("yr", 0, 1), ("yr", 0, -1))
    share(2, 0)
    mail.take(("y", 1, 1, 1))
    share(-1, 1)
    mail.take(("y", 1, 0, -1))
    share(1, 1)
    mail.take(("yr", 1, 1), ("yr", 1, -1))
    share(2, 1)
    xrelay(2)
    mail.finish()


def gather(features, cotangent):
    blocks = jax.ShapeDtypeStruct((32, 128, 128), BF16)
    return pl.pallas_call(
        gather_kernel,
        out_shape=(blocks, blocks),
        in_specs=[VM, VM],
        out_specs=(VM, VM),
        scratch_shapes=[
            pltpu.SemaphoreType.DMA((GATHER_COPIES,)),
            pltpu.SemaphoreType.DMA((GATHER_COPIES,)),
        ],
        compiler_params=pltpu.CompilerParams(collective_id=0, has_side_effects=True),
        name="gather_both",
    )(features, cotangent)


def tile_kernel(rows, cols, live, x_ref, c_ref, w_ref, v_hbm, p_ref, q_ref, g_ref, v_buf, acc_p, acc_q, grad_t, sems):
    blocks = x_ref.shape[0]
    slots = v_hbm.shape[0]
    chunks = sems.shape[0]
    per = slots // chunks
    count = live[0]

    def fetch(i):
        part = pl.ds(i * per, per)
        return pltpu.make_async_copy(v_hbm.at[part], v_buf.at[part], sems.at[i])

    for i in range(chunks):
        pl.when(i * per < count)(lambda i=i: fetch(i).start())
    weight = w_ref[...]
    for j in range(blocks):
        grad_t[j] = lax.dot_general(
            weight, c_ref[j], (((1,), (1,)), ((), ())), preferred_element_type=F32
        ).astype(BF16)
    acc_p[...] = jnp.zeros_like(acc_p)
    acc_q[...] = jnp.zeros_like(acc_q)

    def group(g, _):
        base = g * UNROLL
        for u in range(UNROLL):
            s = base + u
            r, c = rows[s], cols[s]
            alive = s < count
            block = v_buf[s]
            fwd = jnp.dot(block, x_ref[c], preferred_element_type=F32)
            bwd = jnp.dot(grad_t[r], block, preferred_element_type=F32)
            rt = jnp.where(alive, r, blocks)
            ct = jnp.where(alive, c, blocks)
            acc_p[rt] += fwd
            acc_q[ct] += bwd
        return 0

    groups = per // UNROLL
    for i in range(chunks):
        @pl.when(i * per < count)
        def _():
            fetch(i).wait()
            left = jnp.minimum((count - i * per + UNROLL - 1) // UNROLL, groups)
            lax.fori_loop(i * groups, i * groups + left, group, 0)

    total = jnp.zeros(g_ref.shape, F32)
    for j in range(blocks):
        part = acc_p[j].astype(BF16)
        p_ref[j] = part
        q_ref[j] = acc_q[j].T.astype(BF16)
        total += lax.dot_general(
            part, c_ref[j], (((0,), (0,)), ((), ())), preferred_element_type=F32
        )
    g_ref[...] = total


def tile(rows, cols, live, xs, cs, weight, values):
    blocks = jax.ShapeDtypeStruct(xs.shape, BF16)
    n, b, f = xs.shape
    slots = values.shape[0]
    chunks = 10 if slots % (10 * UNROLL) == 0 else 1
    return pl.pallas_call(
        tile_kernel,
        out_shape=(blocks, blocks, jax.ShapeDtypeStruct((f, f), F32)),
        grid_spec=pltpu.PrefetchScalarGridSpec(
            num_scalar_prefetch=3,
            in_specs=[VM, VM, VM, pl.BlockSpec(memory_space=pl.ANY)],
            out_specs=(VM, VM, VM),
            scratch_shapes=[
                pltpu.VMEM((slots, b, b), BF16),
                pltpu.VMEM((n + 1, b, f), F32),
                pltpu.VMEM((n + 1, f, b), F32),
                pltpu.VMEM((n, f, b), BF16),
                pltpu.SemaphoreType.DMA((chunks,)),
            ],
        ),
        compiler_params=pltpu.CompilerParams(vmem_limit_bytes=40 * 1024 * 1024),
        name="tile_products",
    )(rows, cols, live, xs, cs, weight, values)


SCATTER_COPIES = 24 + 6 + 8 + 12 + 1 + (1 + 3 + 3 + 1 + 3 + 3 + 1)


def scatter_kernel(scale, p_ref, q_ref, g_ref, w_ref, out_ref, wg_ref, fg_ref,
                   xr_buf, x_buf, xs_buf, zr_buf, z_buf, zs_buf, s_buf,
                   k_buf, t_buf, yr_buf, y_buf, ys_buf, u_buf, l_buf,
                   gk_buf, gx_buf, gy_buf, gl_buf, gz_buf, gs_buf, send_sems, recv_sems):
    where = place()
    y, l, k, x, z = where
    dev = functools.partial(device, where)
    xp, xm, zp, zm = dev(dx=1), dev(dx=-1), dev(dz=1), dev(dz=-1)
    yp, ym, lo, other = dev(dy=1), dev(dy=-1), dev(dl=1), dev(dc=1)
    meet([xp, xm, zp, zm, yp, ym, lo, other, dev(dx=2), dev(dy=2), dev(dz=2)])
    mail = Mail(send_sems, recv_sems)

    def pat(dx, dz, h):
        return p_ref.at[(((x + dx + 4) % 4) * 4 + (z + dz + 4) % 4) * 2 + h]

    def chip(dy, dl):
        return ((y + dy + 4) % 4) * 2 + (l + dl) % 2

    def add(*refs):
        total = refs[0][...].astype(F32)
        for ref in refs[1:]:
            total = total + ref[...].astype(F32)
        return total

    def xrelay(d):
        i = d % 4
        mail.send(("xr", d, 1), pat(2, d, 0), xr_buf.at[i, 0], xp)
        mail.send(("xr", d, -1), pat(2, d, 1), xr_buf.at[i, 1], xm)

    def xplain(d):
        i = d % 4
        mail.send(("x", d, 1, 1), pat(1, d, 1), x_buf.at[i, 0, 1], xp)
        mail.send(("x", d, 0, -1), pat(-1, d, 0), x_buf.at[i, 1, 0], xm)

    def xsum(d):
        i = d % 4
        mail.take(("xr", d, 1))
        xs_buf[i, 0] = add(pat(1, d, 0), xr_buf.at[i, 0]).astype(BF16)
        mail.send(("x", d, 0, 1), xs_buf.at[i, 0], x_buf.at[i, 0, 0], xp)
        mail.take(("xr", d, -1))
        xs_buf[i, 1] = add(pat(-1, d, 1), xr_buf.at[i, 1]).astype(BF16)
        mail.send(("x", d, 1, -1), xs_buf.at[i, 1], x_buf.at[i, 1, 1], xm)

    def xtotal(d, h):
        i = d % 4
        mail.take(("x", d, h, 1), ("x", d, h, -1))
        return add(pat(0, d, h), x_buf.at[i, 0, h], x_buf.at[i, 1, h])

    def ksend(dy, dl):
        i = chip(dy, dl)
        mail.send(("k", dy, dl), q_ref.at[i, (k + 1) % 2], k_buf.at[i], other)

    def ktake(dy, dl):
        i = chip(dy, dl)
        mail.take(("k", dy, dl))
        t_buf[i] = add(q_ref.at[i, k], k_buf.at[i]).astype(BF16)

    def yrelay(e):
        i = chip(2, e)
        mail.send(("yr", e, 1), t_buf.at[i, 0], yr_buf.at[e, 0], yp)
        mail.send(("yr", e, -1), t_buf.at[i, 1], yr_buf.at[e, 1], ym)

    def yplain(e):
        mail.send(("y", e, 1, 1), t_buf.at[chip(1, e), 1], y_buf.at[e, 0, 1], yp)
        mail.send(("y", e, 0, -1), t_buf.at[chip(-1, e), 0], y_buf.at[e, 1, 0], ym)

    def ysum(e):
        mail.take(("yr", e, 1))
        ys_buf[e, 0] = add(t_buf.at[chip(1, e), 0], yr_buf.at[e, 0]).astype(BF16)
        mail.send(("y", e, 0, 1), ys_buf.at[e, 0], y_buf.at[e, 0, 0], yp)
        mail.take(("yr", e, -1))
        ys_buf[e, 1] = add(t_buf.at[chip(-1, e), 1], yr_buf.at[e, 1]).astype(BF16)
        mail.send(("y", e, 1, -1), ys_buf.at[e, 1], y_buf.at[e, 1, 1], ym)

    def ytotal(e, h):
        mail.take(("y", e, h, 1), ("y", e, h, -1))
        return add(t_buf.at[chip(0, e), h], y_buf.at[e, 0, h], y_buf.at[e, 1, h])

    half, piece = 64, 16
    mine = pl.multiple_of(k * half, half)
    theirs = pl.multiple_of((1 - k) * half, half)
    mail.send(("gk",), g_ref.at[pl.ds(theirs, half)], gk_buf, other)
    for d in (2, 1, -1, 0):
        xrelay(d)
    for dl in (1, 0):
        for dy in (2, 1, -1, 0):
            ksend(dy, dl)
    xplain(2)

    mail.take(("gk",))
    gs_buf[0] = g_ref[pl.ds(mine, half)] + gk_buf[...]
    for d in (1, 2, 3):
        to = (x + d) % 4
        mail.send(("gx", d), gs_buf.at[0, pl.ds(pl.multiple_of(to * piece, piece), piece)],
                  gx_buf.at[x], dev(dx=d))
    gx_buf[x] = gs_buf[0, pl.ds(pl.multiple_of(x * piece, piece), piece)]

    ktake(2, 1)
    yrelay(1)
    xsum(2)
    xplain(1)
    ktake(1, 1)
    ktake(-1, 1)
    yplain(1)
    ktake(0, 1)
    ktake(2, 0)
    yrelay(0)
    xsum(1)
    xplain(-1)
    mail.take(("gx", 1), ("gx", 2), ("gx", 3))
    gy_buf[y] = (gx_buf[0] + gx_buf[1]) + (gx_buf[2] + gx_buf[3])
    for d in (1, 2, 3):
        mail.send(("gy", d), gy_buf.at[y], gy_buf.at[y], dev(dy=d))
    ktake(1, 0)
    ktake(-1, 0)
    yplain(0)
    ktake(0, 0)
    ysum(1)
    xsum(-1)
    xplain(0)
    ysum(0)
    xsum(0)

    s_buf[2, 0] = xtotal(2, 0).astype(BF16)
    mail.send(("zr", 1), s_buf.at[2, 0], zr_buf.at[0], zp)
    s_buf[2, 1] = xtotal(2, 1).astype(BF16)
    mail.send(("zr", -1), s_buf.at[2, 1], zr_buf.at[1], zm)
    mail.take(("gy", 1), ("gy", 2), ("gy", 3))
    gl_buf[l] = (gy_buf[0] + gy_buf[1]) + (gy_buf[2] + gy_buf[3])
    mail.send(("gl",), gl_buf.at[l], gl_buf.at[l], lo)
    s_buf[1, 1] = xtotal(1, 1).astype(BF16)
    mail.send(("z", 1, 1), s_buf.at[1, 1], z_buf.at[0, 1], zp)
    s_buf[3, 0] = xtotal(-1, 0).astype(BF16)
    mail.send(("z", 0, -1), s_buf.at[3, 0], z_buf.at[1, 0], zm)
    for h in range(2):
        u_buf[h] = ytotal(1, h).astype(BF16)
    mail.send(("l",), u_buf, l_buf, lo)
    mail.take(("gl",))
    gz_buf[z] = gl_buf[0] + gl_buf[1]
    for d in (1, 2, 3):
        mail.send(("gz", d), gz_buf.at[z], gz_buf.at[z], dev(dz=d))
    total = xtotal(1, 0)
    mail.take(("zr", 1))
    zs_buf[0] = (total + zr_buf[0].astype(F32)).astype(BF16)
    mail.send(("z", 0, 1), zs_buf.at[0], z_buf.at[0, 0], zp)
    total = xtotal(-1, 1)
    mail.take(("zr", -1))
    zs_buf[1] = (total + zr_buf[1].astype(F32)).astype(BF16)
    mail.send(("z", 1, -1), zs_buf.at[1], z_buf.at[1, 1], zm)

    mail.take(("gz", 1), ("gz", 2), ("gz", 3))
    place_x = pl.ds(pl.multiple_of(k * half + x * piece, piece), piece)
    wg_sum = ((gz_buf[0] + gz_buf[1]) + (gz_buf[2] + gz_buf[3])) * scale
    gs_buf[1, pl.ds(pl.multiple_of(x * piece, piece), piece)] = wg_sum
    for d in (1, 2, 3):
        mine_x = gs_buf.at[1, pl.ds(pl.multiple_of(x * piece, piece), piece)]
        mail.send(("ga", d), mine_x, mine_x, dev(dx=d))
    mail.take(("l",))
    for h in range(2):
        fg_ref[h] = (ytotal(0, h) + l_buf[h].astype(F32)).astype(BF16)
    mail.take(("ga", 1), ("ga", 2), ("ga", 3))
    mail.send(("gb",), gs_buf.at[1], wg_ref.at[pl.ds(mine, half)], other)
    wg_ref[pl.ds(mine, half)] = gs_buf[1]

    for h in range(2):
        total = xtotal(0, h)
        mail.take(("z", h, 1), ("z", h, -1))
        agg = (total + z_buf[0, h].astype(F32) + z_buf[1, h].astype(F32)).astype(BF16)
        out_ref[h] = jnp.dot(agg, w_ref[...], preferred_element_type=F32).astype(BF16)
    mail.finish()


def scatter(ps, qs, grads, weight, scale):
    b = ps.shape[1:]
    own = jax.ShapeDtypeStruct((2, *b), BF16)
    half = lambda *lead: pltpu.VMEM((*lead, *b), BF16)
    piece = lambda n: pltpu.VMEM((n, 16, 128), F32)
    return pl.pallas_call(
        functools.partial(scatter_kernel, scale),
        out_shape=(own, jax.ShapeDtypeStruct(grads.shape, F32), own),
        in_specs=[VM] * 4,
        out_specs=(VM,) * 3,
        scratch_shapes=[
            half(4, 2), half(4, 2, 2), half(4, 2), half(2), half(2, 2), half(2), half(4, 2),
            half(8, 2), half(8, 2), half(2, 2), half(2, 2, 2), half(2, 2), half(2), half(2),
            pltpu.VMEM((64, 128), F32), piece(4), piece(4), piece(2), piece(4),
            pltpu.VMEM((2, 64, 128), F32),
            pltpu.SemaphoreType.DMA((SCATTER_COPIES,)),
            pltpu.SemaphoreType.DMA((SCATTER_COPIES,)),
        ],
        compiler_params=pltpu.CompilerParams(collective_id=1, has_side_effects=True),
        name="scatter_both",
    )(ps, qs.reshape(8, 2, 2, *b), grads, weight)


def local(features, block_values, block_row, block_col, block_occupancy, weight, cotangent):
    width = features.shape[2]
    block = block_values.shape[3]
    nodes = lax.axis_size("row") * lax.axis_size("col") * features.shape[1]
    xs, cs = gather(features.reshape(-1, block, width), cotangent.reshape(-1, block, width))
    ps, qs, grads = tile(
        block_row[0, 0], block_col[0, 0], block_occupancy[0], xs, cs, weight, block_values[0, 0]
    )
    out, wgrad, fgrad = scatter(ps, qs, grads, weight, 1.0 / math.sqrt(nodes))
    return (out.reshape(features.shape), wgrad, fgrad.reshape(features.shape))


def solution(mesh):
    in_specs = (
        P("col", "row", None),
        P("row", "col", None, None, None),
        P("row", "col", None),
        P("row", "col", None),
        P("row", "col"),
        P(),
        P("row", "col", None),
    )
    out_specs = (P("row", "col", None), P(), P("col", "row", None))
    return jax.shard_map(local, mesh=mesh, in_specs=in_specs, out_specs=out_specs, check_vma=False)
```

```python
import functools
import math

import jax
import jax.numpy as jnp
from jax import lax
from jax.experimental import pallas as pl
from jax.experimental.pallas import tpu as pltpu
from jax.sharding import PartitionSpec as P

MESH = pl.DeviceIdType.MESH
F32 = jnp.float32
BF16 = jnp.bfloat16
I32 = jnp.int32
VM = pl.BlockSpec(memory_space=pltpu.VMEM)
LANES = 128
BLOCKS = 32
SLOTS = 320
LISTED = 384
PAIRS = (SLOTS + BLOCKS) // 2
UNROLL = 8
CHUNKS = 10
NONE = 99
FAR = 4096


def turned(row):
    return jnp.broadcast_to(row, (LANES, LANES)).T


def list_pairs(tab, base, keys, others):
    down = lax.broadcasted_iota(I32, (LANES, LANES), 0)
    across = lax.broadcasted_iota(I32, (LANES, LANES), 1)
    parts = range(len(keys))
    kc = [turned(key) for key in keys]
    xc = [turned(other) for other in others]
    count = lambda mask, what=1: jnp.sum(jnp.where(mask, what, 0), axis=0, keepdims=True)
    ranks, lows, odds = [], [], []
    for a in parts:
        rank = low = same = jnp.zeros((1, LANES), I32)
        for b in parts:
            equal = kc[b] == keys[a]
            same += count(equal)
            low += count(kc[b] < keys[a])
            if b < a:
                rank += count(equal)
            elif b == a:
                rank += count(equal & (down < across))
        ranks.append(rank)
        lows.append(low)
        odds.append(jnp.where((rank == 0) & (same % 2 == 1), 1, 0))
    oc = [turned(odd) for odd in odds]
    pc = []
    for a in parts:
        spot = ranks[a] + lows[a]
        for b in parts:
            spot += count(kc[b] < keys[a], oc[b])
        pc.append(turned(jnp.where(keys[a] >= BLOCKS, FAR, spot)))
    for q in parts:
        slot = jnp.full((1, LANES), SLOTS, I32)
        other = jnp.zeros((1, LANES), I32)
        key = jnp.full((1, LANES), NONE, I32)
        for b in parts:
            hit = pc[b] == across + q * LANES
            slot += count(hit, down + (b * LANES - SLOTS))
            other += count(hit, xc[b])
            key += count(hit, kc[b] - NONE)
        part = pl.ds(q * LANES, LANES)
        tab[base : base + 1, part] = slot
        tab[base + 1 : base + 2, part] = other
        tab[base + 2 : base + 3, part] = key
    top = jnp.zeros((1, LANES), I32)
    for b in parts:
        spots = jnp.where(kc[b] == across, pc[b] + 1, 0)
        top = jnp.maximum(top, jnp.max(spots, axis=0, keepdims=True))
    tab[base + 3 : base + 4, 0:LANES] = jnp.where(top == 0, PAIRS, (top - 1) // 2)


def make_lists(tab, pad, rows_ref, cols_ref, live):
    slot = lax.broadcasted_iota(I32, (1, SLOTS), 1)
    pad[...] = jnp.full(pad.shape, BLOCKS, I32)
    pad[0:1, 0:SLOTS] = jnp.where(slot < live, rows_ref[...], BLOCKS)
    pad[1:2, 0:SLOTS] = jnp.where(slot < live, cols_ref[...], BLOCKS)
    split = lambda i: [pad[i : i + 1, a * LANES : (a + 1) * LANES] for a in range(LISTED // LANES)]
    rows, cols = split(0), split(1)
    list_pairs(tab, 0, rows, cols)
    list_pairs(tab, 4, cols, rows)


def pair_sums(tab, base, first, last, acc, sums, product):
    def step(g, acc):
        for u in range(UNROLL):
            i = g * UNROLL + u
            a, b = 2 * i, 2 * i + 1
            made = product(tab[base, a], tab[base + 1, a], tab[base, b], tab[base + 1, b])
            before = tab[base + 2, jnp.maximum(a - 2, 0)]
            keep = (tab[base + 2, a] == before) & (i > 0)
            acc = jnp.where(keep, acc, 0.0) + made
            sums[i] = acc.astype(BF16)
        return acc

    return lax.fori_loop(first // UNROLL, last // UNROLL, step, acc)


def forward_product(v_buf, x_all, s1, c1, s2, c2):
    left = jnp.concatenate((v_buf[s1], v_buf[s2]), axis=1)
    right = jnp.concatenate((x_all[c1], x_all[c2]), axis=0)
    return jnp.dot(left, right, preferred_element_type=F32)


def backward_product(v_buf, grad_t, s1, r1, s2, r2):
    left = jnp.concatenate((grad_t[r1], grad_t[r2]), axis=1)
    right = jnp.concatenate((v_buf[s1], v_buf[s2]), axis=0)
    return jnp.dot(left, right, preferred_element_type=F32)


def place():
    r, c = lax.axis_index("row"), lax.axis_index("col")
    return r // 4, (r // 2) % 2, r % 2, c // 4, c % 4


def device(where, dy=0, dl=0, dc=0, dx=0, dz=0):
    y, l, k, x, z = where
    row = ((y + dy + 4) % 4) * 4 + ((l + dl) % 2) * 2 + (k + dc) % 2
    col = ((x + dx + 4) % 4) * 4 + (z + dz + 4) % 4
    return (row, col)


def meet(peers):
    barrier = pltpu.get_barrier_semaphore()
    for peer in peers:
        pl.semaphore_signal(barrier, inc=1, device_id=peer, device_id_type=MESH)
    pl.semaphore_wait(barrier, len(peers))


class Mail:
    def __init__(self, send_sems, recv_sems):
        self.send_sems, self.recv_sems = send_sems, recv_sems
        self.copies, self.waiting = {}, {}

    def send(self, key, src, dst, peer):
        i = len(self.copies)
        copy = pltpu.make_async_remote_copy(
            src_ref=src,
            dst_ref=dst,
            send_sem=self.send_sems.at[i],
            recv_sem=self.recv_sems.at[i],
            device_id=peer,
            device_id_type=MESH,
        )
        copy.start()
        self.copies[key] = copy
        self.waiting[key] = copy

    def take(self, *keys):
        for key in keys:
            if key in self.waiting:
                self.waiting.pop(key).wait_recv()

    def finish(self):
        self.take(*list(self.waiting))
        for copy in self.copies.values():
            copy.wait_send()


GATHER_COPIES = 6 + 24 + 1 + 10 + 8
SCATTER_COPIES = 24 + 6 + 8 + 6 + 1
GRAD_COPIES = 45
COPIES = GATHER_COPIES + SCATTER_COPIES + GRAD_COPIES
RING = ((0, 1), (1, -1), (1, 1), (0, -1))


def layer_kernel(f_ref, c_ref, w_ref, rows_ref, cols_ref, live_ref, v_hbm,
                 agg_ref, wg_ref, fg_ref,
                 f_all, c_all, v_buf, sums, grad_t, p_buf, q_buf, grad, tab, pad, tab_s,
                 xr_buf, x_buf, xs_buf, zr_buf, z_buf, zs_buf, s_buf,
                 k_buf, t_buf, y_buf, u_buf, l_buf, g1_buf, g2_buf, g3_buf,
                 v_sems, tab_sem, send_sems, recv_sems):
    per = SLOTS // CHUNKS
    loads = []
    for i in range(CHUNKS):
        part = pl.ds(i * per, per)
        loads.append(pltpu.make_async_copy(v_hbm.at[part], v_buf.at[part], v_sems.at[i]))
        loads[-1].start()

    where = place()
    y, l, k, x, z = where
    dev = functools.partial(device, where)
    xp, xm, zp, zm = dev(dx=1), dev(dx=-1), dev(dz=1), dev(dz=-1)
    yp, ym, y2, lo, other = dev(dy=1), dev(dy=-1), dev(dy=2), dev(dl=1), dev(dc=1)
    meet([xp, xm, zp, zm, yp, ym, y2, lo, other])
    mail = Mail(send_sems, recv_sems)

    def at(dx, dz):
        return ((x + dx + 4) % 4) * 4 + (z + dz + 4) % 4

    def cat(dx, dz, h):
        return c_all.at[at(dx, dz) * 2 + h]

    def fat(dy, dl):
        return f_all.at[pl.ds((((y + dy + 4) % 4) * 4 + ((l + dl) % 2) * 2 + k) * 2, 2)]

    def xsend(d, h, p):
        src = c_ref.at[h] if d == 0 else cat(0, d, h)
        mail.send(("ax", d, h, p), src, cat(0, d, h), xp if p > 0 else xm)

    def zsend(h, p):
        mail.send(("az", h, p), c_ref.at[h], cat(0, 0, h), zp if p > 0 else zm)

    def ysend(e):
        src = f_ref if e == 0 else fat(0, e)
        for dy, peer in ((1, yp), (-1, ym), (2, y2)):
            mail.send(("ay", e, dy), src, fat(0, e), peer)

    def relay(d):
        mail.take(("ax", d, 0, 1))
        mail.send(("axr", d, 1), cat(-1, d, 0), cat(-1, d, 0), xp)
        mail.take(("ax", d, 1, -1))
        mail.send(("axr", d, -1), cat(1, d, 1), cat(1, d, 1), xm)

    def share(dy, dl):
        mail.send(("ak", dy, dl), f_ref if (dy, dl) == (0, 0) else fat(dy, dl), fat(dy, dl), other)

    for h, p in RING:
        zsend(h, p)
        xsend(0, h, p)
        if (h, p) == (0, 1):
            mail.send(("al",), f_ref, fat(0, 0), lo)
    ysend(0)
    share(0, 0)
    c_all[pl.ds(at(0, 0) * 2, 2)] = c_ref[...]
    f_all[pl.ds((y * 4 + l * 2 + k) * 2, 2)] = f_ref[...]
    v_buf[SLOTS] = jnp.zeros(v_buf.shape[1:], BF16)
    sums[PAIRS] = jnp.zeros(sums.shape[1:], BF16)
    make_lists(tab, pad, rows_ref, cols_ref, live_ref[0, 0])
    to_scalars = pltpu.make_async_copy(tab, tab_s, tab_sem)
    to_scalars.start()

    mail.take(("al",))
    ysend(1)
    relay(0)
    mail.take(("az", 0, 1))
    mail.send(("azr", 1), cat(0, -1, 0), cat(0, -1, 0), zp)
    xsend(-1, 0, 1)
    xsend(-1, 0, -1)
    mail.take(("az", 1, -1))
    mail.send(("azr", -1), cat(0, 1, 1), cat(0, 1, 1), zm)
    xsend(1, 1, 1)
    xsend(1, 1, -1)
    mail.take(("az", 1, 1))
    xsend(-1, 1, 1)
    xsend(-1, 1, -1)
    mail.take(("az", 0, -1))
    xsend(1, 0, 1)
    xsend(1, 0, -1)
    share(0, 1)
    for dy in (1, -1, 2):
        mail.take(("ay", 0, dy))
        share(-dy, 0)
    relay(-1)
    mail.take(("azr", 1))
    xsend(2, 0, 1)
    xsend(2, 0, -1)
    mail.take(("azr", -1))
    xsend(2, 1, 1)
    xsend(2, 1, -1)
    relay(1)
    for dy in (1, -1, 2):
        mail.take(("ay", 1, dy))
        share(-dy, 1)
    to_scalars.wait()
    for load in loads:
        load.wait()
    mail.take(*[key for key in list(mail.waiting) if key[0] == "ak"])

    zero = jnp.zeros((LANES, LANES), F32)
    fwd = functools.partial(forward_product, v_buf, f_all)
    acc = pair_sums(tab_s, 0, 0, FIRST, zero, sums, fwd)
    relay(2)
    pair_sums(tab_s, 0, FIRST, PAIRS, acc, sums, fwd)

    def pat(dx, dz, h):
        return p_buf.at[at(dx, dz) * 2 + h]

    def chip(dy, dl):
        return ((y + dy + 4) % 4) * 2 + (l + dl) % 2

    def add(*refs):
        total = refs[0][...].astype(F32)
        for ref in refs[1:]:
            total = total + ref[...].astype(F32)
        return total

    def xrelay(d):
        i = d % 4
        mail.send(("xr", d, 1), pat(2, d, 0), xr_buf.at[i, 0], xp)
        mail.send(("xr", d, -1), pat(2, d, 1), xr_buf.at[i, 1], xm)

    def xplain(d):
        i = d % 4
        mail.send(("x", d, 1, 1), pat(1, d, 1), x_buf.at[i, 0, 1], xp)
        mail.send(("x", d, 0, -1), pat(-1, d, 0), x_buf.at[i, 1, 0], xm)

    def xsum(d):
        i = d % 4
        mail.take(("xr", d, 1))
        xs_buf[i, 0] = add(pat(1, d, 0), xr_buf.at[i, 0]).astype(BF16)
        mail.send(("x", d, 0, 1), xs_buf.at[i, 0], x_buf.at[i, 0, 0], xp)
        mail.take(("xr", d, -1))
        xs_buf[i, 1] = add(pat(-1, d, 1), xr_buf.at[i, 1]).astype(BF16)
        mail.send(("x", d, 1, -1), xs_buf.at[i, 1], x_buf.at[i, 1, 1], xm)

    def xtotal(d, h):
        i = d % 4
        mail.take(("x", d, h, 1), ("x", d, h, -1))
        return add(pat(0, d, h), x_buf.at[i, 0, h], x_buf.at[i, 1, h])

    def ksend(dy, dl):
        i = chip(dy, dl)
        mail.send(("k", dy, dl), q_buf.at[i, (k + 1) % 2], k_buf.at[i], other)

    def ktake(dy, dl):
        i = chip(dy, dl)
        mail.take(("k", dy, dl))
        t_buf[i] = add(q_buf.at[i, k], k_buf.at[i]).astype(BF16)

    def yscatter(e, dy, peer):
        mail.send(("y", e, dy), t_buf.at[chip(dy, e)], y_buf.at[e, dy % 4 - 1], peer)

    def ytotal(e):
        for dy in (1, -1, 2):
            mail.take(("y", e, dy))
        return add(t_buf.at[chip(0, e)], *[y_buf.at[e, i] for i in range(3)])

    for r in range(BLOCKS):
        p_buf[r] = sums[tab_s[3, r]]
    for d in (2, 1, -1, 0):
        xrelay(d)
    xplain(2)

    mail.take(*[key for key in list(mail.waiting) if key[0] in ("ax", "axr")])
    total = zero
    weight = w_ref[...]
    for r in range(BLOCKS):
        total += lax.dot_general(
            p_buf[r], c_all[r], (((0,), (0,)), ((), ())), preferred_element_type=F32
        )
    for i in range(16):
        grad[i] = total[8 * i : 8 * i + 8]
    g_row, g_col = y * 4 + l * 2 + k, x * 4 + z
    g1_buf[g_row] = grad[g_row]
    others = [(dy, dl, dc) for dy in range(4) for dl in range(2) for dc in range(2)][1:]
    for dy, dl, dc in others:
        to = ((y + dy) % 4) * 4 + ((l + dl) % 2) * 2 + (k + dc) % 2
        mail.send(("g1", dy, dl, dc), grad.at[to], g1_buf.at[g_row], dev(dy=dy, dl=dl, dc=dc))
    for r in range(BLOCKS):
        grad_t[r] = lax.dot_general(
            weight, c_all[r], (((1,), (1,)), ((), ())), preferred_element_type=F32
        ).astype(BF16)

    bwd = functools.partial(backward_product, v_buf, grad_t)
    acc = pair_sums(tab_s, 4, 0, FIRST, zero, sums, bwd)
    xsum(2)
    xplain(1)
    mail.take(*[("g1", *o) for o in others])
    g2_buf[g_col] = functools.reduce(jnp.add, [g1_buf[i] for i in range(16)])
    far = [(dx, dz) for dx in range(4) for dz in range(4)][1:]
    for dx, dz in far:
        mail.send(("g2", dx, dz), g2_buf.at[g_col], g2_buf.at[g_col], dev(dx=dx, dz=dz))
    xsum(1)
    xplain(-1)
    pair_sums(tab_s, 4, FIRST, PAIRS, acc, sums, bwd)

    for c in range(BLOCKS):
        q_buf[c // 4, (c // 2) % 2, c % 2] = sums[tab_s[7, c]].astype(F32).T.astype(BF16)
    for dl in (1, 0):
        for dy in (2, 1, -1, 0):
            ksend(dy, dl)
    xsum(-1)
    xplain(0)
    xsum(0)
    for e in (1, 0):
        for dy, peer in ((2, y2), (1, yp), (-1, ym)):
            ktake(dy, e)
            yscatter(e, dy, peer)
        ktake(0, e)

    s_buf[2, 0] = xtotal(2, 0).astype(BF16)
    mail.send(("zr", 1), s_buf.at[2, 0], zr_buf.at[0], zp)
    s_buf[2, 1] = xtotal(2, 1).astype(BF16)
    mail.send(("zr", -1), s_buf.at[2, 1], zr_buf.at[1], zm)
    s_buf[1, 1] = xtotal(1, 1).astype(BF16)
    mail.send(("z", 1, 1), s_buf.at[1, 1], z_buf.at[0, 1], zp)
    s_buf[3, 0] = xtotal(-1, 0).astype(BF16)
    mail.send(("z", 0, -1), s_buf.at[3, 0], z_buf.at[1, 0], zm)
    mail.take(*[("g2", *o) for o in far])
    g3_buf[g_row] = functools.reduce(jnp.add, [g2_buf[i] for i in range(16)])
    for dy, dl, dc in others:
        mail.send(("g3", dy, dl, dc), g3_buf.at[g_row], g3_buf.at[g_row], dev(dy=dy, dl=dl, dc=dc))
    total = xtotal(1, 0)
    mail.take(("zr", 1))
    zs_buf[0] = (total + zr_buf[0].astype(F32)).astype(BF16)
    mail.send(("z", 0, 1), zs_buf.at[0], z_buf.at[0, 0], zp)
    total = xtotal(-1, 1)
    mail.take(("zr", -1))
    zs_buf[1] = (total + zr_buf[1].astype(F32)).astype(BF16)
    mail.send(("z", 1, -1), zs_buf.at[1], z_buf.at[1, 1], zm)

    u_buf[...] = ytotal(1).astype(BF16)
    mail.send(("l",), u_buf, l_buf, lo)
    mine = ytotal(0)
    for h in range(2):
        total = xtotal(0, h)
        mail.take(("z", h, 1), ("z", h, -1))
        agg_ref[h] = (total + z_buf[0, h].astype(F32) + z_buf[1, h].astype(F32)).astype(BF16)
    mail.take(*[("g3", *o) for o in others])
    for i in range(16):
        wg_ref[8 * i : 8 * i + 8] = g3_buf[i]
    mail.take(("l",))
    fg_ref[...] = (mine + l_buf[...].astype(F32)).astype(BF16)
    mail.finish()


FIRST = 11 * UNROLL


def layer(features, cotangent, weight, rows, cols, live, values):
    b = (LANES, LANES)
    blocks = lambda *lead: pltpu.VMEM((*lead, *b), BF16)
    own = jax.ShapeDtypeStruct((2, *b), BF16)
    piece = pltpu.VMEM((16, 8, LANES), F32)
    return pl.pallas_call(
        layer_kernel,
        out_shape=(own, jax.ShapeDtypeStruct(b, F32), own),
        in_specs=[VM, VM, VM, VM, VM, pl.BlockSpec(memory_space=pltpu.SMEM), pl.BlockSpec(memory_space=pl.ANY)],
        out_specs=(VM,) * 3,
        scratch_shapes=[
            blocks(BLOCKS), blocks(BLOCKS), blocks(SLOTS + 1), blocks(PAIRS + 1), blocks(BLOCKS),
            blocks(BLOCKS), blocks(8, 2, 2), piece,
            pltpu.VMEM((8, LISTED), I32), pltpu.VMEM((8, LISTED), I32), pltpu.SMEM((8, LISTED), I32),
            blocks(4, 2), blocks(4, 2, 2), blocks(4, 2), blocks(2), blocks(2, 2), blocks(2), blocks(4, 2),
            blocks(8, 2), blocks(8, 2), blocks(2, 3, 2), blocks(2), blocks(2),
            piece, piece, piece,
            pltpu.SemaphoreType.DMA((CHUNKS,)), pltpu.SemaphoreType.DMA(()),
            pltpu.SemaphoreType.DMA((COPIES,)), pltpu.SemaphoreType.DMA((COPIES,)),
        ],
        compiler_params=pltpu.CompilerParams(
            collective_id=0, has_side_effects=True, vmem_limit_bytes=48 * 1024 * 1024
        ),
        name="layer",
    )(features, cotangent, weight, rows, cols, live, values)


def finish_kernel(scale, agg_ref, w_ref, g_ref, fg_ref, out_ref, wg_ref, f_ref):
    out_ref[...] = jnp.dot(agg_ref[...], w_ref[...], preferred_element_type=F32).astype(BF16)
    wg_ref[...] = g_ref[...] * scale
    f_ref[...] = fg_ref[...]


def finish(agg, weight, grad, fgrad, scale):
    shapes = [jax.ShapeDtypeStruct(a.shape, a.dtype) for a in (agg, grad, fgrad)]
    return pl.pallas_call(
        functools.partial(finish_kernel, scale),
        out_shape=shapes,
        in_specs=[VM] * 4,
        out_specs=[VM] * 3,
        name="finish",
    )(agg, weight, grad, fgrad)


def local(features, block_values, block_row, block_col, block_occupancy, weight, cotangent):
    width = features.shape[2]
    block = block_values.shape[3]
    nodes = lax.axis_size("row") * lax.axis_size("col") * features.shape[1]
    agg, grad, fgrad = layer(
        features.reshape(-1, block, width), cotangent.reshape(-1, block, width), weight,
        block_row[0], block_col[0], block_occupancy, block_values[0, 0],
    )
    out, wgrad, fgrad = finish(
        agg.reshape(-1, width), weight, grad, fgrad.reshape(-1, width), 1.0 / math.sqrt(nodes)
    )
    return (out.reshape(features.shape), wgrad, fgrad.reshape(features.shape))


def solution(mesh):
    in_specs = (
        P("col", "row", None),
        P("row", "col", None, None, None),
        P("row", "col", None),
        P("row", "col", None),
        P("row", "col"),
        P(),
        P("row", "col", None),
    )
    out_specs = (P("row", "col", None), P(), P("col", "row", None))
    return jax.shard_map(local, mesh=mesh, in_specs=in_specs, out_specs=out_specs, check_vma=False)
```

```python
import functools
import math

import jax
import jax.numpy as jnp
from jax import lax
from jax.experimental import pallas as pl
from jax.experimental.pallas import tpu as pltpu
from jax.sharding import PartitionSpec as P

MESH = pl.DeviceIdType.MESH
F32 = jnp.float32
BF16 = jnp.bfloat16
I32 = jnp.int32
VM = pl.BlockSpec(memory_space=pltpu.VMEM)
ANY = pl.BlockSpec(memory_space=pltpu.HBM)
LANES = 128
BLOCKS = 32
SLOTS = 320
LISTED = 384
PAIRS = (SLOTS + BLOCKS) // 2
UNROLL = 8
CHUNKS = 10
NONE = 99
FAR = 4096


def turned(row):
    return jnp.broadcast_to(row, (LANES, LANES)).T


def list_pairs(tab, base, keys, others):
    down = lax.broadcasted_iota(I32, (LANES, LANES), 0)
    across = lax.broadcasted_iota(I32, (LANES, LANES), 1)
    parts = range(len(keys))
    kc = [turned(key) for key in keys]
    xc = [turned(other) for other in others]
    count = lambda mask, what=1: jnp.sum(jnp.where(mask, what, 0), axis=0, keepdims=True)
    ranks, lows, odds = [], [], []
    for a in parts:
        rank = low = same = jnp.zeros((1, LANES), I32)
        for b in parts:
            equal = kc[b] == keys[a]
            same += count(equal)
            low += count(kc[b] < keys[a])
            if b < a:
                rank += count(equal)
            elif b == a:
                rank += count(equal & (down < across))
        ranks.append(rank)
        lows.append(low)
        odds.append(jnp.where((rank == 0) & (same % 2 == 1), 1, 0))
    oc = [turned(odd) for odd in odds]
    pc = []
    for a in parts:
        spot = ranks[a] + lows[a]
        for b in parts:
            spot += count(kc[b] < keys[a], oc[b])
        pc.append(turned(jnp.where(keys[a] >= BLOCKS, FAR, spot)))
    for q in parts:
        slot = jnp.full((1, LANES), SLOTS, I32)
        other = jnp.zeros((1, LANES), I32)
        key = jnp.full((1, LANES), NONE, I32)
        for b in parts:
            hit = pc[b] == across + q * LANES
            slot += count(hit, down + (b * LANES - SLOTS))
            other += count(hit, xc[b])
            key += count(hit, kc[b] - NONE)
        part = pl.ds(q * LANES, LANES)
        tab[base : base + 1, part] = slot
        tab[base + 1 : base + 2, part] = other
        tab[base + 2 : base + 3, part] = key
    top = jnp.zeros((1, LANES), I32)
    for b in parts:
        spots = jnp.where(kc[b] == across, pc[b] + 1, 0)
        top = jnp.maximum(top, jnp.max(spots, axis=0, keepdims=True))
    tab[base + 3 : base + 4, 0:LANES] = jnp.where(top == 0, PAIRS, (top - 1) // 2)


def make_lists(tab, pad, rows_ref, cols_ref, live):
    slot = lax.broadcasted_iota(I32, (1, SLOTS), 1)
    pad[...] = jnp.full(pad.shape, BLOCKS, I32)
    pad[0:1, 0:SLOTS] = jnp.where(slot < live, rows_ref[...], BLOCKS)
    pad[1:2, 0:SLOTS] = jnp.where(slot < live, cols_ref[...], BLOCKS)
    split = lambda i: [pad[i : i + 1, a * LANES : (a + 1) * LANES] for a in range(LISTED // LANES)]
    rows, cols = split(0), split(1)
    list_pairs(tab, 0, rows, cols)
    list_pairs(tab, 4, cols, rows)


def pair_sums(tab, base, first, last, acc, sums, product):
    def step(g, acc):
        for u in range(UNROLL):
            i = g * UNROLL + u
            a, b = 2 * i, 2 * i + 1
            made = product(tab[base, a], tab[base + 1, a], tab[base, b], tab[base + 1, b])
            before = tab[base + 2, jnp.maximum(a - 2, 0)]
            keep = (tab[base + 2, a] == before) & (i > 0)
            acc = jnp.where(keep, acc, 0.0) + made
            sums[i] = acc.astype(BF16)
        return acc

    return lax.fori_loop(first // UNROLL, last // UNROLL, step, acc)


def forward_product(v_buf, x_all, s1, c1, s2, c2):
    left = jnp.concatenate((v_buf[s1], v_buf[s2]), axis=1)
    right = jnp.concatenate((x_all[c1], x_all[c2]), axis=0)
    return jnp.dot(left, right, preferred_element_type=F32)


def backward_product(v_buf, grad_t, s1, r1, s2, r2):
    left = jnp.concatenate((grad_t[r1], grad_t[r2]), axis=1)
    right = jnp.concatenate((v_buf[s1], v_buf[s2]), axis=0)
    return jnp.dot(left, right, preferred_element_type=F32)


def place():
    r, c = lax.axis_index("row"), lax.axis_index("col")
    return r // 4, (r // 2) % 2, r % 2, c // 4, c % 4


def device(where, dy=0, dl=0, dc=0, dx=0, dz=0):
    y, l, k, x, z = where
    row = ((y + dy + 4) % 4) * 4 + ((l + dl) % 2) * 2 + (k + dc) % 2
    col = ((x + dx + 4) % 4) * 4 + (z + dz + 4) % 4
    return (row, col)


def meet(peers):
    barrier = pltpu.get_barrier_semaphore()
    for peer in peers:
        pl.semaphore_signal(barrier, inc=1, device_id=peer, device_id_type=MESH)
    pl.semaphore_wait(barrier, len(peers))


class Mail:
    def __init__(self, send_sems, recv_sems):
        self.send_sems, self.recv_sems = send_sems, recv_sems
        self.copies, self.waiting = {}, {}

    def send(self, key, src, dst, peer):
        i = len(self.copies)
        copy = pltpu.make_async_remote_copy(
            src_ref=src,
            dst_ref=dst,
            send_sem=self.send_sems.at[i],
            recv_sem=self.recv_sems.at[i],
            device_id=peer,
            device_id_type=MESH,
        )
        copy.start()
        self.copies[key] = copy
        self.waiting[key] = copy

    def take(self, *keys):
        for key in keys:
            if key in self.waiting:
                self.waiting.pop(key).wait_recv()

    def finish(self):
        self.take(*list(self.waiting))
        for copy in self.copies.values():
            copy.wait_send()


GATHER_COPIES = 6 + 24 + 1 + 10 + 8
SCATTER_COPIES = 24 + 6 + 8 + 6 + 1
GRAD_COPIES = 45
COPIES = GATHER_COPIES + SCATTER_COPIES + GRAD_COPIES
RING = ((0, 1), (1, -1), (1, 1), (0, -1))


def layer_kernel(f_hbm, c_hbm, w_hbm, rows_hbm, cols_hbm, live_ref, v_hbm,
                 agg_ref, wg_ref, fg_ref,
                 w_ref, rows_ref, cols_ref, f_all, c_all, v_buf, sums, grad_t, p_buf, q_buf, grad, tab, pad, tab_s,
                 xr_buf, x_buf, xs_buf, zr_buf, z_buf, zs_buf, s_buf,
                 k_buf, t_buf, y_buf, u_buf, l_buf, g1_buf, g2_buf, g3_buf,
                 in_sems, v_sems, tab_sem, send_sems, recv_sems):
    where = place()
    y, l, k, x, z = where
    g_row, g_col = y * 4 + l * 2 + k, x * 4 + z
    f_own, c_own = f_all.at[pl.ds(g_row * 2, 2)], c_all.at[pl.ds(g_col * 2, 2)]
    pairs = ((c_hbm, c_own), (f_hbm, f_own), (rows_hbm, rows_ref), (cols_hbm, cols_ref), (w_hbm, w_ref))
    inputs = [pltpu.make_async_copy(src, dst, in_sems.at[i]) for i, (src, dst) in enumerate(pairs)]
    for copy in inputs:
        copy.start()
    per = SLOTS // CHUNKS
    loads = []
    for i in range(CHUNKS):
        part = pl.ds(i * per, per)
        loads.append(pltpu.make_async_copy(v_hbm.at[part], v_buf.at[part], v_sems.at[i]))
        loads[-1].start()
    dev = functools.partial(device, where)
    xp, xm, zp, zm = dev(dx=1), dev(dx=-1), dev(dz=1), dev(dz=-1)
    yp, ym, y2, lo, other = dev(dy=1), dev(dy=-1), dev(dy=2), dev(dl=1), dev(dc=1)
    meet([xp, xm, zp, zm, yp, ym, y2, lo, other])
    mail = Mail(send_sems, recv_sems)
    for copy in inputs:
        copy.wait()

    def at(dx, dz):
        return ((x + dx + 4) % 4) * 4 + (z + dz + 4) % 4

    def cat(dx, dz, h):
        return c_all.at[at(dx, dz) * 2 + h]

    def fat(dy, dl):
        return f_all.at[pl.ds((((y + dy + 4) % 4) * 4 + ((l + dl) % 2) * 2 + k) * 2, 2)]

    def xsend(d, h, p):
        mail.send(("ax", d, h, p), cat(0, d, h), cat(0, d, h), xp if p > 0 else xm)

    def zsend(h, p):
        mail.send(("az", h, p), cat(0, 0, h), cat(0, 0, h), zp if p > 0 else zm)

    def ysend(e):
        for dy, peer in ((1, yp), (-1, ym), (2, y2)):
            mail.send(("ay", e, dy), fat(0, e), fat(0, e), peer)

    def relay(d):
        mail.take(("ax", d, 0, 1))
        mail.send(("axr", d, 1), cat(-1, d, 0), cat(-1, d, 0), xp)
        mail.take(("ax", d, 1, -1))
        mail.send(("axr", d, -1), cat(1, d, 1), cat(1, d, 1), xm)

    def share(dy, dl):
        mail.send(("ak", dy, dl), fat(dy, dl), fat(dy, dl), other)

    for h, p in RING:
        zsend(h, p)
        xsend(0, h, p)
        if (h, p) == (0, 1):
            mail.send(("al",), fat(0, 0), fat(0, 0), lo)
    ysend(0)
    share(0, 0)
    v_buf[SLOTS] = jnp.zeros(v_buf.shape[1:], BF16)
    sums[PAIRS] = jnp.zeros(sums.shape[1:], BF16)
    make_lists(tab, pad, rows_ref, cols_ref, live_ref[0, 0])
    to_scalars = pltpu.make_async_copy(tab, tab_s, tab_sem)
    to_scalars.start()

    mail.take(("al",))
    ysend(1)
    relay(0)
    mail.take(("az", 0, 1))
    mail.send(("azr", 1), cat(0, -1, 0), cat(0, -1, 0), zp)
    xsend(-1, 0, 1)
    xsend(-1, 0, -1)
    mail.take(("az", 1, -1))
    mail.send(("azr", -1), cat(0, 1, 1), cat(0, 1, 1), zm)
    xsend(1, 1, 1)
    xsend(1, 1, -1)
    mail.take(("az", 1, 1))
    xsend(-1, 1, 1)
    xsend(-1, 1, -1)
    mail.take(("az", 0, -1))
    xsend(1, 0, 1)
    xsend(1, 0, -1)
    share(0, 1)
    for dy in (1, -1, 2):
        mail.take(("ay", 0, dy))
        share(-dy, 0)
    relay(-1)
    mail.take(("azr", 1))
    xsend(2, 0, 1)
    xsend(2, 0, -1)
    mail.take(("azr", -1))
    xsend(2, 1, 1)
    xsend(2, 1, -1)
    relay(1)
    for dy in (1, -1, 2):
        mail.take(("ay", 1, dy))
        share(-dy, 1)
    to_scalars.wait()
    for load in loads:
        load.wait()
    mail.take(*[key for key in list(mail.waiting) if key[0] == "ak"])

    zero = jnp.zeros((LANES, LANES), F32)
    fwd = functools.partial(forward_product, v_buf, f_all)
    acc = pair_sums(tab_s, 0, 0, FIRST, zero, sums, fwd)
    relay(2)
    pair_sums(tab_s, 0, FIRST, PAIRS, acc, sums, fwd)

    def pat(dx, dz, h):
        return p_buf.at[at(dx, dz) * 2 + h]

    def chip(dy, dl):
        return ((y + dy + 4) % 4) * 2 + (l + dl) % 2

    def add(*refs):
        total = refs[0][...].astype(F32)
        for ref in refs[1:]:
            total = total + ref[...].astype(F32)
        return total

    def xrelay(d):
        i = d % 4
        mail.send(("xr", d, 1), pat(2, d, 0), xr_buf.at[i, 0], xp)
        mail.send(("xr", d, -1), pat(2, d, 1), xr_buf.at[i, 1], xm)

    def xplain(d):
        i = d % 4
        mail.send(("x", d, 1, 1), pat(1, d, 1), x_buf.at[i, 0, 1], xp)
        mail.send(("x", d, 0, -1), pat(-1, d, 0), x_buf.at[i, 1, 0], xm)

    def xsum(d):
        i = d % 4
        mail.take(("xr", d, 1))
        xs_buf[i, 0] = add(pat(1, d, 0), xr_buf.at[i, 0]).astype(BF16)
        mail.send(("x", d, 0, 1), xs_buf.at[i, 0], x_buf.at[i, 0, 0], xp)
        mail.take(("xr", d, -1))
        xs_buf[i, 1] = add(pat(-1, d, 1), xr_buf.at[i, 1]).astype(BF16)
        mail.send(("x", d, 1, -1), xs_buf.at[i, 1], x_buf.at[i, 1, 1], xm)

    def xtotal(d, h):
        i = d % 4
        mail.take(("x", d, h, 1), ("x", d, h, -1))
        return add(pat(0, d, h), x_buf.at[i, 0, h], x_buf.at[i, 1, h])

    def ksend(dy, dl):
        i = chip(dy, dl)
        mail.send(("k", dy, dl), q_buf.at[i, (k + 1) % 2], k_buf.at[i], other)

    def ktake(dy, dl):
        i = chip(dy, dl)
        mail.take(("k", dy, dl))
        t_buf[i] = add(q_buf.at[i, k], k_buf.at[i]).astype(BF16)

    def yscatter(e, dy, peer):
        mail.send(("y", e, dy), t_buf.at[chip(dy, e)], y_buf.at[e, dy % 4 - 1], peer)

    def ytotal(e):
        for dy in (1, -1, 2):
            mail.take(("y", e, dy))
        return add(t_buf.at[chip(0, e)], *[y_buf.at[e, i] for i in range(3)])

    for r in range(BLOCKS):
        p_buf[r] = sums[tab_s[3, r]]
    for d in (2, 1, -1, 0):
        xrelay(d)
    xplain(2)

    mail.take(*[key for key in list(mail.waiting) if key[0] in ("ax", "axr")])
    total = zero
    weight = w_ref[...]
    for r in range(BLOCKS):
        total += lax.dot_general(
            p_buf[r], c_all[r], (((0,), (0,)), ((), ())), preferred_element_type=F32
        )
    for i in range(16):
        grad[i] = total[8 * i : 8 * i + 8]
    g1_buf[g_row] = grad[g_row]
    others = [(dy, dl, dc) for dy in range(4) for dl in range(2) for dc in range(2)][1:]
    for dy, dl, dc in others:
        to = ((y + dy) % 4) * 4 + ((l + dl) % 2) * 2 + (k + dc) % 2
        mail.send(("g1", dy, dl, dc), grad.at[to], g1_buf.at[g_row], dev(dy=dy, dl=dl, dc=dc))
    for r in range(BLOCKS):
        grad_t[r] = lax.dot_general(
            weight, c_all[r], (((1,), (1,)), ((), ())), preferred_element_type=F32
        ).astype(BF16)

    bwd = functools.partial(backward_product, v_buf, grad_t)
    acc = pair_sums(tab_s, 4, 0, FIRST, zero, sums, bwd)
    xsum(2)
    xplain(1)
    mail.take(*[("g1", *o) for o in others])
    g2_buf[g_col] = functools.reduce(jnp.add, [g1_buf[i] for i in range(16)])
    far = [(dx, dz) for dx in range(4) for dz in range(4)][1:]
    for dx, dz in far:
        mail.send(("g2", dx, dz), g2_buf.at[g_col], g2_buf.at[g_col], dev(dx=dx, dz=dz))
    xsum(1)
    xplain(-1)
    pair_sums(tab_s, 4, FIRST, PAIRS, acc, sums, bwd)

    for c in range(BLOCKS):
        q_buf[c // 4, (c // 2) % 2, c % 2] = sums[tab_s[7, c]].astype(F32).T.astype(BF16)
    for dl in (1, 0):
        for dy in (2, 1, -1, 0):
            ksend(dy, dl)
    xsum(-1)
    xplain(0)
    xsum(0)
    for e in (1, 0):
        for dy, peer in ((2, y2), (1, yp), (-1, ym)):
            ktake(dy, e)
            yscatter(e, dy, peer)
        ktake(0, e)

    s_buf[2, 0] = xtotal(2, 0).astype(BF16)
    mail.send(("zr", 1), s_buf.at[2, 0], zr_buf.at[0], zp)
    s_buf[2, 1] = xtotal(2, 1).astype(BF16)
    mail.send(("zr", -1), s_buf.at[2, 1], zr_buf.at[1], zm)
    s_buf[1, 1] = xtotal(1, 1).astype(BF16)
    mail.send(("z", 1, 1), s_buf.at[1, 1], z_buf.at[0, 1], zp)
    s_buf[3, 0] = xtotal(-1, 0).astype(BF16)
    mail.send(("z", 0, -1), s_buf.at[3, 0], z_buf.at[1, 0], zm)
    mail.take(*[("g2", *o) for o in far])
    g3_buf[g_row] = functools.reduce(jnp.add, [g2_buf[i] for i in range(16)])
    for dy, dl, dc in others:
        mail.send(("g3", dy, dl, dc), g3_buf.at[g_row], g3_buf.at[g_row], dev(dy=dy, dl=dl, dc=dc))
    total = xtotal(1, 0)
    mail.take(("zr", 1))
    zs_buf[0] = (total + zr_buf[0].astype(F32)).astype(BF16)
    mail.send(("z", 0, 1), zs_buf.at[0], z_buf.at[0, 0], zp)
    total = xtotal(-1, 1)
    mail.take(("zr", -1))
    zs_buf[1] = (total + zr_buf[1].astype(F32)).astype(BF16)
    mail.send(("z", 1, -1), zs_buf.at[1], z_buf.at[1, 1], zm)

    u_buf[...] = ytotal(1).astype(BF16)
    mail.send(("l",), u_buf, l_buf, lo)
    mine = ytotal(0)
    for h in range(2):
        total = xtotal(0, h)
        mail.take(("z", h, 1), ("z", h, -1))
        agg_ref[h] = (total + z_buf[0, h].astype(F32) + z_buf[1, h].astype(F32)).astype(BF16)
    mail.take(*[("g3", *o) for o in others])
    for i in range(16):
        wg_ref[8 * i : 8 * i + 8] = g3_buf[i]
    mail.take(("l",))
    fg_ref[...] = (mine + l_buf[...].astype(F32)).astype(BF16)
    mail.finish()


FIRST = 11 * UNROLL


def layer(features, cotangent, weight, rows, cols, live, values):
    b = (LANES, LANES)
    blocks = lambda *lead: pltpu.VMEM((*lead, *b), BF16)
    own = jax.ShapeDtypeStruct((2, *b), BF16)
    piece = pltpu.VMEM((16, 8, LANES), F32)
    return pl.pallas_call(
        layer_kernel,
        out_shape=(own, jax.ShapeDtypeStruct(b, F32), own),
        in_specs=[ANY, ANY, ANY, ANY, ANY, pl.BlockSpec(memory_space=pltpu.SMEM), ANY],
        out_specs=(VM,) * 3,
        scratch_shapes=[
            pltpu.VMEM(b, BF16), pltpu.VMEM((1, SLOTS), I32), pltpu.VMEM((1, SLOTS), I32),
            blocks(BLOCKS), blocks(BLOCKS), blocks(SLOTS + 1), blocks(PAIRS + 1), blocks(BLOCKS),
            blocks(BLOCKS), blocks(8, 2, 2), piece,
            pltpu.VMEM((8, LISTED), I32), pltpu.VMEM((8, LISTED), I32), pltpu.SMEM((8, LISTED), I32),
            blocks(4, 2), blocks(4, 2, 2), blocks(4, 2), blocks(2), blocks(2, 2), blocks(2), blocks(4, 2),
            blocks(8, 2), blocks(8, 2), blocks(2, 3, 2), blocks(2), blocks(2),
            piece, piece, piece,
            pltpu.SemaphoreType.DMA((5,)), pltpu.SemaphoreType.DMA((CHUNKS,)), pltpu.SemaphoreType.DMA(()),
            pltpu.SemaphoreType.DMA((COPIES,)), pltpu.SemaphoreType.DMA((COPIES,)),
        ],
        compiler_params=pltpu.CompilerParams(
            collective_id=0, has_side_effects=True, vmem_limit_bytes=67043328
        ),
        name="layer",
    )(features, cotangent, weight, rows, cols, live, values)


def finish_kernel(scale, agg_ref, w_ref, g_ref, fg_ref, out_ref, wg_ref, f_ref):
    out_ref[...] = jnp.dot(agg_ref[...], w_ref[...], preferred_element_type=F32).astype(BF16)
    wg_ref[...] = g_ref[...] * scale
    f_ref[...] = fg_ref[...]


def finish(agg, weight, grad, fgrad, scale):
    shapes = [jax.ShapeDtypeStruct(a.shape, a.dtype) for a in (agg, grad, fgrad)]
    return pl.pallas_call(
        functools.partial(finish_kernel, scale),
        out_shape=shapes,
        in_specs=[VM] * 4,
        out_specs=[VM] * 3,
        compiler_params=pltpu.CompilerParams(vmem_limit_bytes=67043328),
        name="finish",
    )(agg, weight, grad, fgrad)


def local(features, block_values, block_row, block_col, block_occupancy, weight, cotangent):
    width = features.shape[2]
    block = block_values.shape[3]
    nodes = lax.axis_size("row") * lax.axis_size("col") * features.shape[1]
    agg, grad, fgrad = layer(
        features.reshape(-1, block, width), cotangent.reshape(-1, block, width), weight,
        block_row[0], block_col[0], block_occupancy, block_values[0, 0],
    )
    out, wgrad, fgrad = finish(
        agg.reshape(-1, width), weight, grad, fgrad.reshape(-1, width), 1.0 / math.sqrt(nodes)
    )
    return (out.reshape(features.shape), wgrad, fgrad.reshape(features.shape))


def solution(mesh):
    in_specs = (
        P("col", "row", None),
        P("row", "col", None, None, None),
        P("row", "col", None),
        P("row", "col", None),
        P("row", "col"),
        P(),
        P("row", "col", None),
    )
    out_specs = (P("row", "col", None), P(), P("col", "row", None))
    return jax.shard_map(local, mesh=mesh, in_specs=in_specs, out_specs=out_specs, check_vma=False)
```

```python
import functools
import math

import jax
import jax.numpy as jnp
from jax import lax
from jax.experimental import pallas as pl
from jax.experimental.pallas import tpu as pltpu
from jax.sharding import PartitionSpec as P

MESH = pl.DeviceIdType.MESH
F32 = jnp.float32
BF16 = jnp.bfloat16
I32 = jnp.int32
VM = pl.BlockSpec(memory_space=pltpu.VMEM)
ANY = pl.BlockSpec(memory_space=pltpu.HBM)
LANES = 128
BLOCKS = 32
SLOTS = 320
LISTED = 384
PAIRS = (SLOTS + BLOCKS) // 2
UNROLL = 8
CHUNKS = 10
NONE = 99
FAR = 4096


def turned(row):
    return jnp.broadcast_to(row, (LANES, LANES)).T


def list_pairs(tab, base, keys, others):
    down = lax.broadcasted_iota(I32, (LANES, LANES), 0)
    across = lax.broadcasted_iota(I32, (LANES, LANES), 1)
    parts = range(len(keys))
    kc = [turned(key) for key in keys]
    xc = [turned(other) for other in others]
    count = lambda mask, what=1: jnp.sum(jnp.where(mask, what, 0), axis=0, keepdims=True)
    ranks, lows, odds = [], [], []
    for a in parts:
        rank = low = same = jnp.zeros((1, LANES), I32)
        for b in parts:
            equal = kc[b] == keys[a]
            same += count(equal)
            low += count(kc[b] < keys[a])
            if b < a:
                rank += count(equal)
            elif b == a:
                rank += count(equal & (down < across))
        ranks.append(rank)
        lows.append(low)
        odds.append(jnp.where((rank == 0) & (same % 2 == 1), 1, 0))
    oc = [turned(odd) for odd in odds]
    pc = []
    for a in parts:
        spot = ranks[a] + lows[a]
        for b in parts:
            spot += count(kc[b] < keys[a], oc[b])
        pc.append(turned(jnp.where(keys[a] >= BLOCKS, FAR, spot)))
    for q in parts:
        slot = jnp.full((1, LANES), SLOTS, I32)
        other = jnp.zeros((1, LANES), I32)
        key = jnp.full((1, LANES), NONE, I32)
        for b in parts:
            hit = pc[b] == across + q * LANES
            slot += count(hit, down + (b * LANES - SLOTS))
            other += count(hit, xc[b])
            key += count(hit, kc[b] - NONE)
        part = pl.ds(q * LANES, LANES)
        tab[base : base + 1, part] = slot
        tab[base + 1 : base + 2, part] = other
        tab[base + 2 : base + 3, part] = key
    top = jnp.zeros((1, LANES), I32)
    for b in parts:
        spots = jnp.where(kc[b] == across, pc[b] + 1, 0)
        top = jnp.maximum(top, jnp.max(spots, axis=0, keepdims=True))
    tab[base + 3 : base + 4, 0:LANES] = jnp.where(top == 0, PAIRS, (top - 1) // 2)


def live_keys(pad, rows_ref, cols_ref, live):
    slot = lax.broadcasted_iota(I32, (1, SLOTS), 1)
    pad[...] = jnp.full(pad.shape, BLOCKS, I32)
    pad[0:1, 0:SLOTS] = jnp.where(slot < live, rows_ref[...], BLOCKS)
    pad[1:2, 0:SLOTS] = jnp.where(slot < live, cols_ref[...], BLOCKS)
    split = lambda i: [pad[i : i + 1, a * LANES : (a + 1) * LANES] for a in range(LISTED // LANES)]
    rows, cols = split(0), split(1)
    return rows, cols


def pair_sums(tab, base, first, last, acc, sums, product):
    def step(g, acc):
        for u in range(UNROLL):
            i = g * UNROLL + u
            a, b = 2 * i, 2 * i + 1
            made = product(tab[base, a], tab[base + 1, a], tab[base, b], tab[base + 1, b])
            before = tab[base + 2, jnp.maximum(a - 2, 0)]
            keep = (tab[base + 2, a] == before) & (i > 0)
            acc = jnp.where(keep, acc, 0.0) + made
            sums[i] = acc.astype(BF16)
        return acc

    return lax.fori_loop(first // UNROLL, last // UNROLL, step, acc)


def forward_product(v_buf, x_all, s1, c1, s2, c2):
    left = jnp.concatenate((v_buf[s1], v_buf[s2]), axis=1)
    right = jnp.concatenate((x_all[c1], x_all[c2]), axis=0)
    return jnp.dot(left, right, preferred_element_type=F32)


def backward_product(v_buf, grad_t, s1, r1, s2, r2):
    left = jnp.concatenate((grad_t[r1], grad_t[r2]), axis=1)
    right = jnp.concatenate((v_buf[s1], v_buf[s2]), axis=0)
    return jnp.dot(left, right, preferred_element_type=F32)


def place():
    r, c = lax.axis_index("row"), lax.axis_index("col")
    return r // 4, (r // 2) % 2, r % 2, c // 4, c % 4


def device(where, dy=0, dl=0, dc=0, dx=0, dz=0):
    y, l, k, x, z = where
    row = ((y + dy + 4) % 4) * 4 + ((l + dl) % 2) * 2 + (k + dc) % 2
    col = ((x + dx + 4) % 4) * 4 + (z + dz + 4) % 4
    return (row, col)


def meet(peers):
    barrier = pltpu.get_barrier_semaphore()
    for peer in peers:
        pl.semaphore_signal(barrier, inc=1, device_id=peer, device_id_type=MESH)
    pl.semaphore_wait(barrier, len(peers))


class Mail:
    def __init__(self, send_sems, recv_sems):
        self.send_sems, self.recv_sems = send_sems, recv_sems
        self.count, self.sending, self.waiting, self.bursts = 0, {}, {}, {}

    def send(self, key, src, dst, peer):
        i = self.count
        self.count += 1
        copy = pltpu.make_async_remote_copy(
            src_ref=src,
            dst_ref=dst,
            send_sem=self.send_sems.at[i],
            recv_sem=self.recv_sems.at[i],
            device_id=peer,
            device_id_type=MESH,
        )
        copy.start()
        self.sending[key] = copy
        self.waiting[key] = copy

    def take(self, *keys):
        for key in keys:
            if key in self.waiting:
                self.waiting.pop(key).wait_recv()

    def burst(self, key, whole, items):
        i = self.count
        self.count += 1
        for src, dst, peer in items:
            pltpu.make_async_remote_copy(
                src_ref=src,
                dst_ref=dst,
                send_sem=self.send_sems.at[i],
                recv_sem=self.recv_sems.at[i],
                device_id=peer,
                device_id_type=MESH,
            ).start()
        self.bursts[key] = (i, whole.at[pl.ds(0, len(items))])

    def drain(self, key):
        i, part = self.bursts[key]
        pltpu.make_async_copy(part, part, self.recv_sems.at[i]).wait()

    def settle_bursts(self):
        for i, part in self.bursts.values():
            pltpu.make_async_copy(part, part, self.send_sems.at[i]).wait()

    def settle(self, *kinds):
        for key in list(self.sending):
            if not kinds or key[0] in kinds:
                self.sending.pop(key).wait_send()

    def finish(self):
        self.take(*list(self.waiting))
        self.settle()
        self.settle_bursts()


GATHER_COPIES = 6 + 24 + 2 + 12 + 8
SCATTER_COPIES = 3 + 18 + 6 + 8 + 6 + 1
GRAD_COPIES = 3
COPIES = GATHER_COPIES + SCATTER_COPIES + GRAD_COPIES
RING = ((0, 1), (1, -1), (1, 1), (0, -1))


def layer_kernel(f_hbm, c_hbm, w_hbm, rows_hbm, cols_hbm, live_ref, v_hbm,
                 agg_ref, wg_ref, fg_ref,
                 w_ref, rows_ref, cols_ref, f_all, c_all, v_buf, sums, grad_t, p_buf, q_buf, grad, row_tab, col_tab, pad, row_tab_s, col_tab_s,
                 xr_buf, x_buf, xs_buf, xf_buf, zr_buf, z_buf, s_buf,
                 k_buf, t_buf, y_buf, u_buf, l_buf, g1_buf, g2_buf, g3_buf,
                 in_sems, v_sems, tab_sems, send_sems, recv_sems):
    where = place()
    y, l, k, x, z = where
    g_row, g_col = y * 4 + l * 2 + k, x * 4 + z
    f_own, c_own = f_all.at[pl.ds(g_row * 2, 2)], c_all.at[pl.ds(g_col * 2, 2)]
    pairs = ((c_hbm, c_own), (f_hbm, f_own), (rows_hbm, rows_ref), (cols_hbm, cols_ref), (w_hbm, w_ref))
    inputs = [pltpu.make_async_copy(src, dst, in_sems.at[i]) for i, (src, dst) in enumerate(pairs)]
    for copy in inputs:
        copy.start()
    dev = functools.partial(device, where)
    xp, xm, zp, zm = dev(dx=1), dev(dx=-1), dev(dz=1), dev(dz=-1)
    yp, ym, y2, lo, other = dev(dy=1), dev(dy=-1), dev(dy=2), dev(dl=1), dev(dc=1)
    meet([xp, xm, zp, zm, yp, ym, y2, lo, other])
    mail = Mail(send_sems, recv_sems)
    for copy in inputs:
        copy.wait()

    def at(dx, dz):
        return ((x + dx + 4) % 4) * 4 + (z + dz + 4) % 4

    def cat(dx, dz, h):
        return c_all.at[at(dx, dz) * 2 + h]

    def fat(dy, dl):
        return f_all.at[pl.ds((((y + dy + 4) % 4) * 4 + ((l + dl) % 2) * 2 + k) * 2, 2)]

    def xsend(d, h, p):
        mail.send(("ax", d, h, p), cat(0, d, h), cat(0, d, h), xp if p > 0 else xm)

    def zsend(h, p):
        mail.send(("az", h, p), cat(0, 0, h), cat(0, 0, h), zp if p > 0 else zm)

    def fhalf(dy, dl, h):
        return f_all.at[(((y + dy + 4) % 4) * 4 + ((l + dl) % 2) * 2 + k) * 2 + h]

    def ysend(e, h):
        for dy, peer in ((2, y2), (1, yp), (-1, ym)):
            mail.send(("ay", e, dy, h), fhalf(0, e, h), fhalf(0, e, h), peer)

    def relay(d):
        mail.take(("ax", d, 0, 1))
        mail.send(("axr", d, 1), cat(-1, d, 0), cat(-1, d, 0), xp)
        mail.take(("ax", d, 1, -1))
        mail.send(("axr", d, -1), cat(1, d, 1), cat(1, d, 1), xm)

    def share(dy, dl):
        mail.send(("ak", dy, dl), fat(dy, dl), fat(dy, dl), other)

    for h in range(2):
        mail.send(("al", h), fhalf(0, 0, h), fhalf(0, 0, h), lo)
    for h, p in RING:
        zsend(h, p)
        xsend(0, h, p)
    for h in range(2):
        ysend(0, h)
    share(0, 0)
    v_buf[SLOTS] = jnp.zeros(v_buf.shape[1:], BF16)
    sums[PAIRS] = jnp.zeros(sums.shape[1:], BF16)
    rows, cols = live_keys(pad, rows_ref, cols_ref, live_ref[0, 0])
    list_pairs(row_tab, 0, rows, cols)
    row_scalars = pltpu.make_async_copy(row_tab, row_tab_s, tab_sems.at[0])
    row_scalars.start()

    for h in range(2):
        mail.take(("al", h))
        ysend(1, h)
    share(0, 1)
    relay(0)
    per = SLOTS // CHUNKS
    loads = []
    for i in range(CHUNKS):
        part = pl.ds(i * per, per)
        loads.append(pltpu.make_async_copy(v_hbm.at[part], v_buf.at[part], v_sems.at[i]))
        loads[-1].start()
    mail.take(("az", 0, 1))
    mail.send(("azr", 1), cat(0, -1, 0), cat(0, -1, 0), zp)
    xsend(-1, 0, 1)
    xsend(-1, 0, -1)
    mail.take(("az", 1, -1))
    mail.send(("azr", -1), cat(0, 1, 1), cat(0, 1, 1), zm)
    xsend(1, 1, 1)
    xsend(1, 1, -1)
    mail.take(("az", 1, 1))
    xsend(-1, 1, 1)
    xsend(-1, 1, -1)
    mail.take(("az", 0, -1))
    xsend(1, 0, 1)
    xsend(1, 0, -1)
    for dy in (1, -1, 2):
        mail.take(("ay", 0, dy, 0), ("ay", 0, dy, 1))
        share(-dy, 0)
    list_pairs(col_tab, 0, cols, rows)
    col_scalars = pltpu.make_async_copy(col_tab, col_tab_s, tab_sems.at[1])
    col_scalars.start()
    for dy in (1, -1, 2):
        mail.take(("ay", 1, dy, 0), ("ay", 1, dy, 1))
        share(-dy, 1)
    relay(-1)
    relay(1)
    for h, p in ((0, 1), (1, -1)):
        mail.take(("azr", p))
        xsend(2, h, 1)
        xsend(2, h, -1)
        mail.send(("axf", h), cat(0, 2, h), cat(0, 2, h), dev(dx=2))
    row_scalars.wait()
    col_scalars.wait()
    for load in loads:
        load.wait()
    mail.take(*[key for key in list(mail.waiting) if key[0] == "ak"])

    zero = jnp.zeros((LANES, LANES), F32)
    fwd = functools.partial(forward_product, v_buf, f_all)
    pair_sums(row_tab_s, 0, 0, PAIRS, zero, sums, fwd)

    def pat(dx, dz, h):
        return p_buf.at[at(dx, dz) * 2 + h]

    def chip(dy, dl):
        return ((y + dy + 4) % 4) * 2 + (l + dl) % 2

    def add(*refs):
        total = refs[0][...].astype(F32)
        for ref in refs[1:]:
            total = total + ref[...].astype(F32)
        return total

    def xrelay(d):
        i = d % 4
        mail.send(("xr", d, 1), pat(2, d, 0), xr_buf.at[i, 0], xp)
        mail.send(("xr", d, -1), pat(2, d, 1), xr_buf.at[i, 1], xm)

    def xplain(d):
        i = d % 4
        mail.send(("x", d, 1, 1), pat(1, d, 1), x_buf.at[i, 0, 1], xp)
        mail.send(("x", d, 0, -1), pat(-1, d, 0), x_buf.at[i, 1, 0], xm)

    def xsum(d):
        i = d % 4
        mail.take(("xr", d, 1))
        xs_buf[i, 0] = add(pat(1, d, 0), xr_buf.at[i, 0]).astype(BF16)
        mail.send(("x", d, 0, 1), xs_buf.at[i, 0], x_buf.at[i, 0, 0], xp)
        mail.take(("xr", d, -1))
        xs_buf[i, 1] = add(pat(-1, d, 1), xr_buf.at[i, 1]).astype(BF16)
        mail.send(("x", d, 1, -1), xs_buf.at[i, 1], x_buf.at[i, 1, 1], xm)

    def xtotal(d, h):
        i = d % 4
        mail.take(("x", d, h, 1), ("x", d, h, -1))
        return add(pat(0, d, h), x_buf.at[i, 0, h], x_buf.at[i, 1, h])

    def xfar():
        for j, (dx, peer) in enumerate(((1, xp), (-1, xm), (2, dev(dx=2)))):
            src = p_buf.at[pl.ds(at(dx, 2) * 2, 2)]
            mail.send(("xf", dx), src, xf_buf.at[j], peer)

    def zsend_half(d, h, peer):
        mail.send(("z", d, h), s_buf.at[d % 4, h], z_buf.at[0 if d == 1 else 1, h], peer)

    def ksend(dy, dl):
        i = chip(dy, dl)
        mail.send(("k", dy, dl), q_buf.at[i, (k + 1) % 2], k_buf.at[i], other)

    def ktake(dy, dl):
        i = chip(dy, dl)
        mail.take(("k", dy, dl))
        t_buf[i] = add(q_buf.at[i, k], k_buf.at[i]).astype(BF16)

    def yscatter(e, dy, peer):
        mail.send(("y", e, dy), t_buf.at[chip(dy, e)], y_buf.at[e, dy % 4 - 1], peer)

    def ytotal(e):
        for dy in (1, -1, 2):
            mail.take(("y", e, dy))
        return add(t_buf.at[chip(0, e)], *[y_buf.at[e, i] for i in range(3)])

    for r in range(BLOCKS):
        p_buf[r] = sums[row_tab_s[3, r]]
    xrelay(1)
    xrelay(-1)
    xfar()
    xrelay(0)
    xplain(1)
    xplain(-1)
    mail.take(*[key for key in list(mail.waiting) if key[0] in ("ax", "axr", "axf")])
    total = zero
    weight = w_ref[...]
    for r in range(BLOCKS):
        total += lax.dot_general(
            p_buf[r], c_all[r], (((0,), (0,)), ((), ())), preferred_element_type=F32
        )
    for i in range(16):
        grad[i] = total[8 * i : 8 * i + 8]
    g1_buf[g_row] = grad[g_row]
    others = [(dy, dl, dc) for dy in range(4) for dl in range(2) for dc in range(2)][1:]
    items = []
    for dy, dl, dc in others:
        to = ((y + dy) % 4) * 4 + ((l + dl) % 2) * 2 + (k + dc) % 2
        items.append((grad.at[to], g1_buf.at[g_row], dev(dy=dy, dl=dl, dc=dc)))
    mail.burst("g1", g1_buf, items)
    for r in range(BLOCKS):
        grad_t[r] = lax.dot_general(
            weight, c_all[r], (((1,), (1,)), ((), ())), preferred_element_type=F32
        ).astype(BF16)

    bwd = functools.partial(backward_product, v_buf, grad_t)
    acc = pair_sums(col_tab_s, 0, STOPS[0], STOPS[1], zero, sums, bwd)
    acc = pair_sums(col_tab_s, 0, STOPS[1], STOPS[2], acc, sums, bwd)
    xsum(1)
    xsum(-1)
    xplain(0)
    mail.take(("xf", 1), ("xf", -1), ("xf", 2))
    far_part = p_buf.at[pl.ds(at(0, 2) * 2, 2)]
    s_buf[2] = add(far_part, xf_buf.at[0], xf_buf.at[1], xf_buf.at[2]).astype(BF16)
    mail.send(("zr", 1), s_buf.at[2, 0], zr_buf.at[0], zp)
    mail.send(("zr", -1), s_buf.at[2, 1], zr_buf.at[1], zm)
    acc = pair_sums(col_tab_s, 0, STOPS[2], STOPS[3], acc, sums, bwd)
    xsum(0)
    pair_sums(col_tab_s, 0, STOPS[3], STOPS[4], acc, sums, bwd)

    for c in range(BLOCKS):
        q_buf[c // 4, (c // 2) % 2, c % 2] = sums[col_tab_s[3, c]].astype(F32).T.astype(BF16)
    for dl in (1, 0):
        for dy in (2, 1, -1, 0):
            ksend(dy, dl)
    mail.drain("g1")
    g2_buf[g_col] = functools.reduce(jnp.add, [g1_buf[i] for i in range(16)])
    far = [(dx, dz) for dx in range(4) for dz in range(4)][1:]
    piece = g2_buf.at[g_col]
    mail.burst("g2", g2_buf, [(piece, piece, dev(dx=dx, dz=dz)) for dx, dz in far])
    mail.settle("al", "ax", "axr", "axf", "az", "azr", "ay", "ak")
    for dy, peer in ((2, y2), (1, yp), (-1, ym)):
        ktake(dy, 1)
        yscatter(1, dy, peer)
    for d, peer in ((1, zp), (-1, zm)):
        h = 1 if d == 1 else 0
        s_buf[d % 4, h] = xtotal(d, h).astype(BF16)
        zsend_half(d, h, peer)
    for dy, peer in ((2, y2), (1, yp), (-1, ym)):
        ktake(dy, 0)
        yscatter(0, dy, peer)
    ktake(0, 1)
    ktake(0, 0)
    for d, peer in ((1, zp), (-1, zm)):
        h = 0 if d == 1 else 1
        total = xtotal(d, h)
        mail.take(("zr", d))
        s_buf[d % 4, h] = (total + zr_buf[h].astype(F32)).astype(BF16)
        zsend_half(d, h, peer)
    mail.settle("xr", "xf", "x", "zr", "k")
    u_buf[...] = ytotal(1).astype(BF16)
    mail.send(("l",), u_buf, l_buf, lo)
    mail.drain("g2")
    g3_buf[g_row] = functools.reduce(jnp.add, [g2_buf[i] for i in range(16)])
    piece = g3_buf.at[g_row]
    mail.burst("g3", g3_buf, [(piece, piece, dev(dy=dy, dl=dl, dc=dc)) for dy, dl, dc in others])

    mail.settle("y")
    mine = ytotal(0)
    mail.take(*[("z", d, h) for d in (1, -1) for h in (0, 1)])
    for h in range(2):
        total = xtotal(0, h)
        for i in range(2):
            total = total + z_buf[i, h].astype(F32)
        agg_ref[h] = total.astype(BF16)
    mail.drain("g3")
    for i in range(16):
        wg_ref[8 * i : 8 * i + 8] = g3_buf[i]
    mail.take(("l",))
    fg_ref[...] = (mine + l_buf[...].astype(F32)).astype(BF16)
    mail.finish()


STOPS = (0, 6 * UNROLL, 12 * UNROLL, 17 * UNROLL, PAIRS)


def layer(features, cotangent, weight, rows, cols, live, values):
    b = (LANES, LANES)
    blocks = lambda *lead: pltpu.VMEM((*lead, *b), BF16)
    own = jax.ShapeDtypeStruct((2, *b), BF16)
    piece = pltpu.VMEM((16, 8, LANES), F32)
    return pl.pallas_call(
        layer_kernel,
        out_shape=(own, jax.ShapeDtypeStruct(b, F32), own),
        in_specs=[ANY, ANY, ANY, ANY, ANY, pl.BlockSpec(memory_space=pltpu.SMEM), ANY],
        out_specs=(VM,) * 3,
        scratch_shapes=[
            pltpu.VMEM(b, BF16), pltpu.VMEM((1, SLOTS), I32), pltpu.VMEM((1, SLOTS), I32),
            blocks(BLOCKS), blocks(BLOCKS), blocks(SLOTS + 1), blocks(PAIRS + 1), blocks(BLOCKS),
            blocks(BLOCKS), blocks(8, 2, 2), piece,
            pltpu.VMEM((8, LISTED), I32), pltpu.VMEM((8, LISTED), I32), pltpu.VMEM((8, LISTED), I32),
            pltpu.SMEM((8, LISTED), I32), pltpu.SMEM((8, LISTED), I32),
            blocks(4, 2), blocks(4, 2, 2), blocks(4, 2), blocks(3, 2), blocks(2), blocks(2, 2), blocks(4, 2),
            blocks(8, 2), blocks(8, 2), blocks(2, 3, 2), blocks(2), blocks(2),
            piece, piece, piece,
            pltpu.SemaphoreType.DMA((5,)), pltpu.SemaphoreType.DMA((CHUNKS,)), pltpu.SemaphoreType.DMA((2,)),
            pltpu.SemaphoreType.DMA((COPIES,)), pltpu.SemaphoreType.DMA((COPIES,)),
        ],
        compiler_params=pltpu.CompilerParams(
            collective_id=0, has_side_effects=True, vmem_limit_bytes=67043328
        ),
        name="layer",
    )(features, cotangent, weight, rows, cols, live, values)


def finish_kernel(scale, agg_ref, w_ref, g_ref, fg_ref, out_ref, wg_ref, f_ref):
    out_ref[...] = jnp.dot(agg_ref[...], w_ref[...], preferred_element_type=F32).astype(BF16)
    wg_ref[...] = g_ref[...] * scale
    f_ref[...] = fg_ref[...]


def finish(agg, weight, grad, fgrad, scale):
    shapes = [jax.ShapeDtypeStruct(a.shape, a.dtype) for a in (agg, grad, fgrad)]
    return pl.pallas_call(
        functools.partial(finish_kernel, scale),
        out_shape=shapes,
        in_specs=[VM] * 4,
        out_specs=[VM] * 3,
        compiler_params=pltpu.CompilerParams(vmem_limit_bytes=67043328),
        name="finish",
    )(agg, weight, grad, fgrad)


def local(features, block_values, block_row, block_col, block_occupancy, weight, cotangent):
    width = features.shape[2]
    block = block_values.shape[3]
    nodes = lax.axis_size("row") * lax.axis_size("col") * features.shape[1]
    agg, grad, fgrad = layer(
        features.reshape(-1, block, width), cotangent.reshape(-1, block, width), weight,
        block_row[0], block_col[0], block_occupancy, block_values[0, 0],
    )
    out, wgrad, fgrad = finish(
        agg.reshape(-1, width), weight, grad, fgrad.reshape(-1, width), 1.0 / math.sqrt(nodes)
    )
    return (out.reshape(features.shape), wgrad, fgrad.reshape(features.shape))


def solution(mesh):
    in_specs = (
        P("col", "row", None),
        P("row", "col", None, None, None),
        P("row", "col", None),
        P("row", "col", None),
        P("row", "col"),
        P(),
        P("row", "col", None),
    )
    out_specs = (P("row", "col", None), P(), P("col", "row", None))
    return jax.shard_map(local, mesh=mesh, in_specs=in_specs, out_specs=out_specs, check_vma=False)
```
